256 devices in a mesh: dp: 2 (over z_hi), lat: 2 (over core), row: 64 (over z_lo, y, x).
Axes of the slice: x: 4, y: 4, z: 8 (z_hi: 2, z_lo: 4; z = z_hi * 4 + z_lo), core: 2. Of those that a mesh axis runs over, the one named last changes fastest.
Arguments:
- weight: float32 [5120, 16384], P('row', 'lat'), may hold values from -6 to 6
- grads: float32 [2, 5120, 16384], P('dp', 'row', 'lat'), may hold values from -11000 to 11000
- first: float32 [5120, 2, 8192], P('row', 'dp', 'lat'), may hold values from -4 to 4
- second: float32 [5120, 2, 8192], P('row', 'dp', 'lat'), may hold values from 0.04 to 1
Outputs:
- new_weight: float32 [5120, 16384], P('row', 'lat')
- new_first: float32 [5120, 2, 8192], P('row', 'dp', 'lat')
- new_second: float32 [5120, 2, 8192], P('row', 'dp', 'lat')
The draws below stay inside these ranges and needn't reach their ends.
All inputs are finite; a program needn't handle non-finite values.
Results may differ from the reference program's by a relative error of at most 0.00002.
Values sent between devices are 32-bit elements; how exact they have to be, the bound alone decides.
A program may use at most 64 MiB of HBM per device.

```python
import math
import jax
import jax.numpy as jnp
from jax import lax

D = 5120
LAT_DEV = 8192
LATENTS = 16384
N_DP = 2
N_LAT = 2


def draw_grads(key, part):
    keys = jax.random.split(jax.random.fold_in(key, 11), 3)
    base = jnp.clip(jax.random.normal(keys[0], (N_DP, D, LATENTS), jnp.float32), -4.0, 4.0)
    row_rise = 3.0 ** (jnp.arange(D, dtype=jnp.float32) / D)
    col_rise = 3.0 ** (jnp.arange(LATENTS, dtype=jnp.float32) / LATENTS)
    rows = jnp.exp(jax.random.uniform(keys[1], (D,), jnp.float32) * math.log(10.0)) * row_rise
    cols = jnp.exp(jax.random.uniform(keys[2], (LATENTS,), jnp.float32) * math.log(10.0)) * col_rise
    return (base * rows[None, :, None] * cols[None, None, :]).astype(jnp.float32)


def steps_of(rng, extent, shards, low, top_value):
    gain = 1.0
    for axis_at, blocks in shards:
        heights = jax.random.uniform(jax.random.fold_in(jax.random.fold_in(rng, 6), axis_at), (blocks,), jnp.float32, low / len(shards), top_value / len(shards))
        gain = gain * jnp.repeat(jnp.exp(heights), extent[axis_at] // blocks).reshape((-1,) + (1,) * (len(extent) - 1 - axis_at))
    return gain


def centred(own_key, shape, scale, limit, pieces=(), kind=jnp.bfloat16):
    drawn = scale * jax.random.normal(own_key, shape, jnp.float32)
    if pieces:
        drawn = drawn * steps_of(own_key, shape, pieces, -0.22, 0.18)
    return jnp.clip(drawn, -limit, limit).astype(kind)


def setup_inputs(seed: int = 0) -> dict:
    seeds = jax.random.split(jax.random.key(seed), 5)
    weight = centred(seeds[0], (D, LATENTS), 1.0, 6.0, ((0, 64), (1, 2)), jnp.float32)
    grads = draw_grads(jax.random.fold_in(seeds[4], 71), 0)
    first = centred(seeds[2], (D, N_DP, LATENTS // N_DP), 0.3, 4.0, ((0, 64), (1, 2), (2, 2)), jnp.float32)
    second = jnp.clip(jnp.exp(math.log(1.0) - 3.218876 * jax.random.uniform(seeds[3], (D, N_DP, LATENTS // N_DP), jnp.float32) ** steps_of(seeds[3], (D, N_DP, LATENTS // N_DP), ((0, 64), (1, 2), (2, 2)), -0.2, 0.2)), 0.04, 1.0)
    return dict(weight=weight, grads=grads, first=first, second=second)


def pair(matrix):
    width = LAT_DEV // N_DP
    return matrix.reshape(D, N_LAT, N_DP, width).transpose(0, 2, 1, 3).reshape(D, N_DP, N_LAT * width)

def unpair(paired):
    width = LAT_DEV // N_DP
    return paired.reshape(D, N_DP, N_LAT, width).transpose(0, 2, 1, 3).reshape(D, N_LAT * N_DP * width)

def reference(weight, grads, first, second):
    grad = lax.optimization_barrier(jnp.sum(grads, axis=0))
    inner = lax.optimization_barrier(jnp.sum(weight * grad, axis=0))
    length = lax.optimization_barrier(jnp.sum(weight * weight, axis=0))
    projected = grad - (inner / length)[None, :] * weight
    total = jnp.sum(projected * projected)
    spread = jnp.sqrt(total / (D * LATENTS) + 1e-06)
    clip = jnp.minimum(jnp.float32(1.0), 0.5 / spread)
    clipped = pair(clip * projected)
    new_first = 0.9 * first + 0.1 * clipped
    new_second = 0.999 * second + 0.001 * clipped * clipped
    raw = pair(weight) - 0.2 * new_first / (jnp.sqrt(new_second) + 1e-08)
    scaled = raw * lax.rsqrt(lax.optimization_barrier(jnp.sum(raw * raw, axis=0)) / D + 1e-06)[None, :, :]
    return (unpair(scaled), new_first, new_second)
```

```python
import functools

import jax
import jax.numpy as jnp
from jax import lax
from jax.experimental import pallas as pl
from jax.experimental.pallas import tpu as pltpu
from jax.sharding import PartitionSpec as P

MESH = pl.DeviceIdType.MESH
F32 = jnp.float32
PLANE = 16
Z_LO = 4
BLK = 256
ROWS = 8


def each(low, high, body):
    def step(k, carry):
        body(k)
        return carry

    lax.fori_loop(low, high, step, 0)


def comm(
    depth, entries, w_h, g_h, f_h, s_h, nw, nf, ns,
    w_own, w_oth, g_own, g_oth, fv, sv, got1, proj, raw, got2, norms,
    st, rs1, z1, zs, zo, ratio, sa, sb, cst, rs2, z2, scale,
    load, b1s, b1r, b2s, b2r, small_s, small_r,
):
    rows, half = w_own.shape
    chunks, blocks = rows // ROWS, half // BLK
    dp, lat, row = lax.axis_index("dp"), lax.axis_index("lat"), lax.axis_index("row")
    zlo, q = row // PLANE, lax.rem(row, PLANE)
    z8 = dp * Z_LO + zlo
    u = lat * 8 + z8
    own = pl.multiple_of(dp * half, half)
    oth = pl.multiple_of((1 - dp) * half, half)
    partner = (1 - dp, lat, row)

    def in_plane(k):
        return (dp, lat, zlo * PLANE + lax.rem(q + k, PLANE))

    def along_z(k):
        z = lax.rem(z8 + k, 8)
        return (z // Z_LO, lat, lax.rem(z, Z_LO) * PLANE + q)

    def column(k):
        v = lax.rem(u + k, 16)
        z = lax.rem(v, 8)
        return (z // Z_LO, v // 8, lax.rem(z, Z_LO) * PLANE + q)

    def same_half(j):
        return (dp, lat, lax.rem(zlo + j, Z_LO) * PLANE + q)

    def other_half(j):
        return (1 - dp, lat, lax.rem(zlo + j, Z_LO) * PLANE + q)

    def remote(src, dst, s, r, device):
        return pltpu.make_async_remote_copy(
            src_ref=src, dst_ref=dst, send_sem=s, recv_sem=r, device_id=device, device_id_type=MESH
        )

    def fetch(src, dst, i):
        return pltpu.make_async_copy(src, dst, load.at[i])

    fetches = [
        fetch(w_h.at[:, pl.ds(own, half)], w_own, 0),
        fetch(g_h.at[0, :, pl.ds(own, half)], g_own, 1),
        fetch(w_h.at[:, pl.ds(oth, half)], w_oth, 2),
        fetch(g_h.at[0, :, pl.ds(oth, half)], g_oth, 3),
        fetch(f_h.at[:, 0, :], fv, 4),
        fetch(s_h.at[:, 0, :], sv, 5),
    ]
    for f in fetches:
        f.start()

    barrier = pltpu.get_barrier_semaphore()

    def greet(k):
        pl.semaphore_signal(barrier, inc=1, device_id=in_plane(k), device_id_type=MESH)
        pl.semaphore_signal(barrier, inc=1, device_id=column(k), device_id_type=MESH)

    each(1, 16, greet)
    pl.semaphore_wait(barrier, 30)

    def bulk1(i):
        at = pl.ds(pl.multiple_of(i * ROWS, ROWS), ROWS)
        return remote(g_oth.at[at], got1.at[at], b1s.at[i], b1r.at[i], partner)

    def bulk2(i):
        at = pl.ds(pl.multiple_of(i * ROWS, ROWS), ROWS)
        return remote(raw.at[at], got2.at[at], b2s.at[i], b2r.at[i], partner)

    fetches[3].wait()
    each(0, chunks, lambda i: bulk1(i).start())

    fetches[0].wait()
    fetches[1].wait()

    def own_sums(b):
        at = pl.ds(pl.multiple_of(b * BLK, BLK), BLK)
        w = w_own[:, at]
        st[b, 1] = jnp.sum(w * g_own[:, at], axis=0, keepdims=True)
        st[b, 2] = jnp.sum(w * w, axis=0, keepdims=True)

    each(0, blocks, own_sums)
    fetches[2].wait()

    def other_sums(b):
        at = pl.ds(pl.multiple_of(b * BLK, BLK), BLK)
        st[b, 0] = jnp.sum(w_oth[:, at] * g_oth[:, at], axis=0, keepdims=True)

    each(0, blocks, other_sums)

    def scatter(src, dst, stage):
        def copy(k):
            return remote(
                src.at[lax.rem(q + k, PLANE)], dst.at[q],
                small_s.at[stage, k], small_r.at[stage, k], in_plane(k),
            )

        return copy

    def gather(ref, stage):
        def copy(k):
            return remote(ref.at[q], ref.at[q], small_s.at[stage, k], small_r.at[stage, k], in_plane(k))

        return copy

    def run(copy, low, high):
        each(low, high, lambda k: copy(k).start())
        each(low, high, lambda k: copy(k).wait_recv())

    rs1[q] = st[q]
    scatter1 = scatter(st, rs1, 0)
    run(scatter1, 1, PLANE)
    z1[...] = jnp.sum(rs1[...], axis=0)

    def same_copy(j):
        return remote(z1.at[pl.ds(1, 2)], zs.at[zlo], small_s.at[1, j], small_r.at[1, j], same_half(j))

    def other_copy(j):
        return remote(z1.at[pl.ds(0, 1)], zo.at[zlo], small_s.at[1, 8 + j], small_r.at[1, 8 + j], other_half(j))

    zs[zlo] = z1[1:3]
    each(1, Z_LO, lambda j: same_copy(j).start())
    each(0, Z_LO, lambda j: other_copy(j).start())
    each(1, Z_LO, lambda j: same_copy(j).wait_recv())
    each(0, Z_LO, lambda j: other_copy(j).wait_recv())
    same = jnp.sum(zs[...], axis=0)
    inner = same[0] + jnp.sum(zo[...], axis=0)[0]
    ratio[q] = inner / same[1]
    gather1 = gather(ratio, 2)
    run(gather1, 1, PLANE)

    def project(i, total):
        bulk1(i).wait_recv()
        at = pl.ds(pl.multiple_of(i * ROWS, ROWS), ROWS)
        for b in range(blocks):
            cols = pl.ds(b * BLK, BLK)
            p = (g_own[at, cols] + got1[at, cols]) - ratio[b] * w_own[at, cols]
            proj[at, cols] = p
            total = total + p * p
        return total

    total = lax.fori_loop(0, chunks, project, jnp.zeros((ROWS, BLK), F32))
    total = jnp.sum(total, axis=0, keepdims=True)
    sa[q] = total[:, :128] + total[:, 128:]
    gather_a = gather(sa, 3)
    run(gather_a, 1, PLANE)
    sb[u] = jnp.sum(sa[...], axis=0)

    def gather_b(k):
        return remote(sb.at[u], sb.at[u], small_s.at[4, k], small_r.at[4, k], column(k))

    run(gather_b, 1, 16)
    total = jnp.sum(jnp.sum(sb[...], axis=0), axis=1, keepdims=True)
    clip = jnp.minimum(F32(1.0), 0.5 / jnp.sqrt(total / entries + 1e-06))

    fetches[4].wait()
    fetches[5].wait()
    norms[...] = jnp.zeros_like(norms)

    def update(i):
        at = pl.ds(pl.multiple_of(i * ROWS, ROWS), ROWS)
        for b in range(blocks):
            cols = pl.ds(b * BLK, BLK)
            clipped = clip * proj[at, cols]
            first = 0.9 * fv[at, cols] + 0.1 * clipped
            second = 0.999 * sv[at, cols] + 0.001 * clipped * clipped
            nf[at, cols] = first
            ns[at, cols] = second
            r = w_own[at, cols] - 0.2 * first / (jnp.sqrt(second) + 1e-08)
            raw[at, cols] = r
            norms[:, cols] += r * r
        bulk2(i).start()

    each(0, chunks, update)
    for b in range(blocks):
        cst[b] = jnp.sum(norms[:, pl.ds(b * BLK, BLK)], axis=0, keepdims=True)
    rs2[q] = cst[q]
    scatter2 = scatter(cst, rs2, 5)
    run(scatter2, 1, PLANE)
    z2[z8] = jnp.sum(rs2[...], axis=0)

    def gather_z(k):
        return remote(z2.at[z8], z2.at[z8], small_s.at[6, k], small_r.at[6, k], along_z(k))

    run(gather_z, 1, 8)
    for h in range(2):
        whole = jnp.sum(z2[h * Z_LO : (h + 1) * Z_LO], axis=0)
        scale[q, h] = lax.rsqrt(whole / depth + 1e-06)
    gather2 = gather(scale, 7)
    run(gather2, 1, PLANE)

    def finish(src, part, base):
        def step(i):
            at = pl.ds(pl.multiple_of(i * ROWS, ROWS), ROWS)
            for b in range(blocks):
                cols = pl.ds(pl.multiple_of(base + b * BLK, BLK), BLK)
                nw[at, cols] = src[at, pl.ds(b * BLK, BLK)] * scale[b, part]

        return step

    each(0, chunks, finish(raw, dp, own))
    last = finish(got2, 1 - dp, oth)

    def receive(i):
        bulk2(i).wait_recv()
        last(i)

    each(0, chunks, receive)

    each(0, chunks, lambda i: bulk1(i).wait_send())
    each(0, chunks, lambda i: bulk2(i).wait_send())
    for copy in (scatter1, gather1, gather_a, gather_b, scatter2, gather2):
        each(1, PLANE, lambda k: copy(k).wait_send())
    each(1, 8, lambda k: gather_z(k).wait_send())
    each(1, Z_LO, lambda j: same_copy(j).wait_send())
    each(0, Z_LO, lambda j: other_copy(j).wait_send())


def store(nw, nf, ns, nw_h, nf_h, ns_h, sem):
    copies = [
        pltpu.make_async_copy(nw, nw_h, sem.at[0]),
        pltpu.make_async_copy(nf, nf_h.at[:, 0, :], sem.at[1]),
        pltpu.make_async_copy(ns, ns_h.at[:, 0, :], sem.at[2]),
    ]
    for c in copies:
        c.start()
    for c in copies:
        c.wait()


def solution(mesh):
    def step(weight, grads, first, second):
        rows, width = weight.shape
        half = width // mesh.shape["dp"]
        depth = rows * mesh.shape["row"]
        entries = depth * width * mesh.shape["lat"]
        vmem = pl.BlockSpec(memory_space=pltpu.VMEM)
        hbm = pl.BlockSpec(memory_space=pltpu.HBM)
        tile = pltpu.VMEM((rows, half), F32)
        chunks = rows // ROWS
        dma = pltpu.SemaphoreType.DMA
        new_weight, new_first, new_second = pl.pallas_call(
            functools.partial(comm, depth, entries),
            out_shape=(
                jax.ShapeDtypeStruct((rows, width), F32),
                jax.ShapeDtypeStruct((rows, half), F32),
                jax.ShapeDtypeStruct((rows, half), F32),
            ),
            in_specs=[hbm] * 4,
            out_specs=[vmem] * 3,
            scratch_shapes=[
                *[tile] * 10,
                pltpu.VMEM((ROWS, half), F32),
                pltpu.VMEM((PLANE, 3, 1, BLK), F32),
                pltpu.VMEM((PLANE, 3, 1, BLK), F32),
                pltpu.VMEM((3, 1, BLK), F32),
                pltpu.VMEM((Z_LO, 2, 1, BLK), F32),
                pltpu.VMEM((Z_LO, 1, 1, BLK), F32),
                pltpu.VMEM((PLANE, 1, BLK), F32),
                pltpu.VMEM((PLANE, 1, 128), F32),
                pltpu.VMEM((16, 1, 128), F32),
                pltpu.VMEM((PLANE, 1, BLK), F32),
                pltpu.VMEM((PLANE, 1, BLK), F32),
                pltpu.VMEM((8, 1, BLK), F32),
                pltpu.VMEM((PLANE, 2, 1, BLK), F32),
                dma((6,)),
                dma((chunks,)),
                dma((chunks,)),
                dma((chunks,)),
                dma((chunks,)),
                dma((8, 16)),
                dma((8, 16)),
            ],
            compiler_params=pltpu.CompilerParams(
                collective_id=0, has_side_effects=True, vmem_limit_bytes=24 << 20
            ),
        )(*[pltpu.with_memory_space_constraint(a, pltpu.HBM) for a in (weight, grads, first, second)])
        return pl.pallas_call(
            store,
            out_shape=(
                jax.ShapeDtypeStruct(weight.shape, F32),
                jax.ShapeDtypeStruct(first.shape, F32),
                jax.ShapeDtypeStruct(second.shape, F32),
            ),
            in_specs=[vmem] * 3,
            out_specs=[hbm] * 3,
            scratch_shapes=[dma((3,))],
            compiler_params=pltpu.CompilerParams(vmem_limit_bytes=16 << 20),
        )(new_weight, new_first, new_second)

    return jax.shard_map(
        step,
        mesh=mesh,
        in_specs=(P("row", "lat"), P("dp", "row", "lat"), P("row", "dp", "lat"), P("row", "dp", "lat")),
        out_specs=(P("row", "lat"), P("row", "dp", "lat"), P("row", "dp", "lat")),
        check_vma=False,
    )
```

```python
import functools

import jax
import jax.numpy as jnp
from jax import lax
from jax.experimental import pallas as pl
from jax.experimental.pallas import tpu as pltpu
from jax.sharding import PartitionSpec as P

MESH = pl.DeviceIdType.MESH
F32 = jnp.float32
PLANE = 16
Z_LO = 4
BLK = 256
ROWS = 8
HOPS = 4

def each(low, high, body):
    def step(k, carry):
        body(k)
        return carry

    lax.fori_loop(low, high, step, 0)


def comm(
    depth, entries, w_h, g_h, f_h, s_h, nw, nf, ns,
    w_own, w_oth, g_own, g_oth, fv, sv, grad, raw, norms, ring1, ring2,
    st, rs, col, ratio, plane, cst, pn, zn, scale,
    load, b1s, b1r, b2s, b2r, small_s, small_r,
):
    rows, half = w_own.shape
    chunks, blocks = rows // ROWS, half // BLK
    dp, lat, row = lax.axis_index("dp"), lax.axis_index("lat"), lax.axis_index("row")
    zlo, q = row // PLANE, lax.rem(row, PLANE)
    z8 = dp * Z_LO + zlo
    u = lat * 8 + z8
    own = pl.multiple_of(dp * half, half)
    oth = pl.multiple_of((1 - dp) * half, half)

    def in_plane(k):
        return (dp, lat, zlo * PLANE + lax.rem(q + k, PLANE))

    def column(k):
        v = lax.rem(u + k, 16)
        z = lax.rem(v, 8)
        return (z // Z_LO, v // 8, lax.rem(z, Z_LO) * PLANE + q)

    def along_z(k):
        z = lax.rem(z8 + k, 8)
        return (z // Z_LO, lat, lax.rem(z, Z_LO) * PLANE + q)

    onward = along_z(1 + 6 * lat)

    def remote(src, dst, s, r, device):
        return pltpu.make_async_remote_copy(
            src_ref=src, dst_ref=dst, send_sem=s, recv_sem=r, device_id=device, device_id_type=MESH
        )

    def fetch(src, dst, i):
        return pltpu.make_async_copy(src, dst, load.at[i])

    fetches = [
        fetch(w_h.at[:, pl.ds(own, half)], w_own, 0),
        fetch(g_h.at[0, :, pl.ds(own, half)], g_own, 1),
        fetch(w_h.at[:, pl.ds(oth, half)], w_oth, 2),
        fetch(g_h.at[0, :, pl.ds(oth, half)], g_oth, 3),
        fetch(f_h.at[:, 0, :], fv, 4),
        fetch(s_h.at[:, 0, :], sv, 5),
    ]
    for f in fetches:
        f.start()

    barrier = pltpu.get_barrier_semaphore()

    def greet(k):
        pl.semaphore_signal(barrier, inc=1, device_id=in_plane(k), device_id_type=MESH)
        pl.semaphore_signal(barrier, inc=1, device_id=column(k), device_id_type=MESH)

    each(1, 16, greet)

    def rows_of(i):
        return pl.ds(pl.multiple_of(i * ROWS, ROWS), ROWS)

    def bulk1(hop, i):
        at = rows_of(i)
        src = ring1.at[hop - 1, at] if hop else g_h.at[0, at, pl.ds(oth, half)]
        return remote(src, ring1.at[hop, at], b1s.at[hop, i], b1r.at[hop, i], onward)

    def bulk2(hop, i):
        at = rows_of(i)
        src = ring2.at[hop - 1, at] if hop else raw.at[at]
        return remote(src, ring2.at[hop, at], b2s.at[hop, i], b2r.at[hop, i], onward)

    def forward(bulk, hop, low, high):
        def one(i):
            bulk(hop - 1, i).wait_recv()
            bulk(hop, i).start()

        each(low, high, one)

    fetches[0].wait()
    fetches[1].wait()

    def own_sums(b):
        at = pl.ds(pl.multiple_of(b * BLK, BLK), BLK)
        w = w_own[:, at]
        st[b, dp] = jnp.sum(w * g_own[:, at], axis=0, keepdims=True)
        st[b, 2] = jnp.sum(w * w, axis=0, keepdims=True)

    each(0, blocks, own_sums)
    fetches[2].wait()
    fetches[3].wait()

    def other_sums(b):
        at = pl.ds(pl.multiple_of(b * BLK, BLK), BLK)
        st[b, 1 - dp] = jnp.sum(w_oth[:, at] * g_oth[:, at], axis=0, keepdims=True)

    each(0, blocks, other_sums)
    pl.semaphore_wait(barrier, 30)

    each(0, chunks, lambda i: bulk1(0, i).start())

    def scatter(src, dst, stage):
        def copy(k):
            to = lax.rem(q + k, PLANE)
            return remote(src.at[to], dst.at[q], small_s.at[stage, k], small_r.at[stage, k], in_plane(k))

        return copy

    def gather(ref, stage):
        def copy(k):
            return remote(ref.at[q], ref.at[q], small_s.at[stage, k], small_r.at[stage, k], in_plane(k))

        return copy

    def run(copy, low, high):
        each(low, high, lambda k: copy(k).start())
        each(low, high, lambda k: copy(k).wait_recv())

    rs[q] = st[q]
    scatter1 = scatter(st, rs, 0)
    run(scatter1, 1, PLANE)
    col[u, 0:3] = jnp.sum(rs[...], axis=0)
    for hop in range(1, HOPS):
        forward(bulk1, hop, 0, chunks)

    def add_up(i, total):
        bulk1(HOPS - 1, i).wait_recv()
        at = rows_of(i)
        for b in range(blocks):
            cols = pl.ds(b * BLK, BLK)
            p = g_own[at, cols] + ring1[HOPS - 1, at, cols]
            grad[at, cols] = p
            total = total + p * p
        return total

    total = lax.fori_loop(0, chunks, add_up, jnp.zeros((ROWS, BLK), F32))
    col[u, 3] = jnp.sum(total, axis=0, keepdims=True)

    def gather_z(k):
        return remote(col.at[u], col.at[u], small_s.at[1, k], small_r.at[1, k], column(k))

    run(gather_z, 1, 16)
    total = jnp.zeros((1, BLK), F32)
    for core in range(2):
        parts = [jnp.sum(col[pl.ds(core * 8 + h * Z_LO, Z_LO)], axis=0) for h in range(2)]
        for h in range(2):
            inner = parts[0][h] + parts[1][h]
            ratio[core, h] = inner / parts[h][2]
            total += parts[h][3] - inner * ratio[core, h]
    plane[q, 0] = ratio[lat, dp]
    plane[q, 1] = total
    gather1 = gather(plane, 2)
    run(gather1, 1, PLANE)
    total = jnp.sum(jnp.sum(plane[:, 1], axis=0), axis=1, keepdims=True)
    total = jnp.maximum(total, 0.0)
    clip = jnp.minimum(F32(1.0), 0.5 / jnp.sqrt(total / entries + 1e-06))

    fetches[4].wait()
    fetches[5].wait()
    norms[...] = jnp.zeros_like(norms)

    def update(i):
        at = rows_of(i)
        for b in range(blocks):
            cols = pl.ds(b * BLK, BLK)
            w = w_own[at, cols]
            clipped = clip * (grad[at, cols] - plane[b, 0] * w)
            first = 0.9 * fv[at, cols] + 0.1 * clipped
            second = 0.999 * sv[at, cols] + 0.001 * clipped * clipped
            nf[at, cols] = first
            ns[at, cols] = second
            r = w - 0.2 * first / (jnp.sqrt(second) + 1e-08)
            raw[at, cols] = r
            norms[:, cols] += r * r
        bulk2(0, i).start()

    each(0, chunks, update)
    for b in range(blocks):
        cst[b] = jnp.sum(norms[:, pl.ds(b * BLK, BLK)], axis=0, keepdims=True)

    pn[q] = cst[q]
    scatter2 = scatter(cst, pn, 3)
    run(scatter2, 1, PLANE)
    zn[z8] = jnp.sum(pn[...], axis=0)

    def gather_n(k):
        return remote(zn.at[z8], zn.at[z8], small_s.at[4, k], small_r.at[4, k], along_z(k))

    each(1, 8, lambda k: gather_n(k).start())
    forward(bulk2, 1, 0, chunks)
    forward(bulk2, 2, 0, chunks // 2)
    each(1, 8, lambda k: gather_n(k).wait_recv())
    for h in range(2):
        scale[q, h] = lax.rsqrt(jnp.sum(zn[h * Z_LO : (h + 1) * Z_LO], axis=0) / depth + 1e-06)
    gather2 = gather(scale, 5)
    each(1, PLANE, lambda k: gather2(k).start())
    forward(bulk2, 2, chunks // 2, chunks)
    each(1, PLANE, lambda k: gather2(k).wait_recv())

    def finish(src, part, base):
        def step(i):
            at = rows_of(i)
            for b in range(blocks):
                cols = pl.ds(pl.multiple_of(base + b * BLK, BLK), BLK)
                nw[at, cols] = src[at, pl.ds(b * BLK, BLK)] * scale[b, part]

        return step

    each(0, chunks, finish(raw, dp, own))
    forward(bulk2, 3, 0, chunks)
    last = finish(ring2.at[HOPS - 1], 1 - dp, oth)

    def receive(i):
        bulk2(HOPS - 1, i).wait_recv()
        last(i)

    each(0, chunks, receive)

    for hop in range(HOPS):
        each(0, chunks, lambda i: bulk1(hop, i).wait_send())
        each(0, chunks, lambda i: bulk2(hop, i).wait_send())
    for copy in (scatter1, gather_z, gather1, scatter2, gather2):
        each(1, PLANE, lambda k: copy(k).wait_send())
    each(1, 8, lambda k: gather_n(k).wait_send())


def store(nw, nf, ns, nw_h, nf_h, ns_h, sem):
    copies = [
        pltpu.make_async_copy(nw, nw_h, sem.at[0]),
        pltpu.make_async_copy(nf, nf_h.at[:, 0, :], sem.at[1]),
        pltpu.make_async_copy(ns, ns_h.at[:, 0, :], sem.at[2]),
    ]
    for c in copies:
        c.start()
    for c in copies:
        c.wait()


def solution(mesh):
    def step(weight, grads, first, second):
        rows, width = weight.shape
        half = width // mesh.shape["dp"]
        depth = rows * mesh.shape["row"]
        entries = depth * width * mesh.shape["lat"]
        vmem = pl.BlockSpec(memory_space=pltpu.VMEM)
        hbm = pl.BlockSpec(memory_space=pltpu.HBM)
        tile = pltpu.VMEM((rows, half), F32)
        chunks = rows // ROWS
        dma = pltpu.SemaphoreType.DMA
        new_weight, new_first, new_second = pl.pallas_call(
            functools.partial(comm, depth, entries),
            out_shape=(
                jax.ShapeDtypeStruct((rows, width), F32),
                jax.ShapeDtypeStruct((rows, half), F32),
                jax.ShapeDtypeStruct((rows, half), F32),
            ),
            in_specs=[hbm] * 4,
            out_specs=[vmem] * 3,
            scratch_shapes=[
                *[tile] * 8,
                pltpu.VMEM((ROWS, half), F32),
                pltpu.VMEM((HOPS, rows, half), F32),
                pltpu.VMEM((HOPS, rows, half), F32),
                pltpu.VMEM((PLANE, 3, 1, BLK), F32),
                pltpu.VMEM((PLANE, 3, 1, BLK), F32),
                pltpu.VMEM((16, 4, 1, BLK), F32),
                pltpu.VMEM((2, 2, 1, BLK), F32),
                pltpu.VMEM((PLANE, 2, 1, BLK), F32),
                pltpu.VMEM((PLANE, 1, BLK), F32),
                pltpu.VMEM((PLANE, 1, BLK), F32),
                pltpu.VMEM((8, 1, BLK), F32),
                pltpu.VMEM((PLANE, 2, 1, BLK), F32),
                dma((6,)),
                dma((HOPS, chunks)),
                dma((HOPS, chunks)),
                dma((HOPS, chunks)),
                dma((HOPS, chunks)),
                dma((6, 16)),
                dma((6, 16)),
            ],
            compiler_params=pltpu.CompilerParams(
                collective_id=0, has_side_effects=True, vmem_limit_bytes=32 << 20
            ),
        )(*[pltpu.with_memory_space_constraint(a, pltpu.HBM) for a in (weight, grads, first, second)])
        return pl.pallas_call(
            store,
            out_shape=(
                jax.ShapeDtypeStruct(weight.shape, F32),
                jax.ShapeDtypeStruct(first.shape, F32),
                jax.ShapeDtypeStruct(second.shape, F32),
            ),
            in_specs=[vmem] * 3,
            out_specs=[hbm] * 3,
            scratch_shapes=[dma((3,))],
            compiler_params=pltpu.CompilerParams(vmem_limit_bytes=16 << 20),
        )(new_weight, new_first, new_second)

    return jax.shard_map(
        step,
        mesh=mesh,
        in_specs=(P("row", "lat"), P("dp", "row", "lat"), P("row", "dp", "lat"), P("row", "dp", "lat")),
        out_specs=(P("row", "lat"), P("row", "dp", "lat"), P("row", "dp", "lat")),
        check_vma=False,
    )
```

```python
import functools

import jax
import jax.numpy as jnp
from jax import lax
from jax.experimental import pallas as pl
from jax.experimental.pallas import tpu as pltpu
from jax.sharding import PartitionSpec as P

MESH = pl.DeviceIdType.MESH
F32 = jnp.float32
PLANE = 16
Z_LO = 4
BLK = 256
ROWS = 8
HOPS = 4
SPARE = 128

def each(low, high, body):
    def step(k, carry):
        body(k)
        return carry

    lax.fori_loop(low, high, step, 0)


def comm(
    depth, entries, w_h, g_h, f_h, s_h, nw, nf, ns,
    w_own, w_oth, g_own, g_oth, fv, sv, grad, raw, norms, ring1, ring2,
    st, rs, col, ratio, plane, cst, pn, zn, scale, spare,
    load, b1s, b1r, b2s, b2r, small_s, small_r, spare_s, spare_r,
):
    rows, half = w_own.shape
    chunks, blocks = rows // ROWS, half // BLK
    dp, lat, row = lax.axis_index("dp"), lax.axis_index("lat"), lax.axis_index("row")
    zlo, q = row // PLANE, lax.rem(row, PLANE)
    z8 = dp * Z_LO + zlo
    u = lat * 8 + z8
    own = pl.multiple_of(dp * half, half)
    oth = pl.multiple_of((1 - dp) * half, half)

    def in_plane(k):
        return (dp, lat, zlo * PLANE + lax.rem(q + k, PLANE))

    def column(k):
        v = lax.rem(u + k, 16)
        z = lax.rem(v, 8)
        return (z // Z_LO, v // 8, lax.rem(z, Z_LO) * PLANE + q)

    def along_z(k):
        z = lax.rem(z8 + k, 8)
        return (z // Z_LO, lat, lax.rem(z, Z_LO) * PLANE + q)

    onward = along_z(1 + 6 * lat)
    partner = along_z(HOPS)

    def remote(src, dst, s, r, device):
        return pltpu.make_async_remote_copy(
            src_ref=src, dst_ref=dst, send_sem=s, recv_sem=r, device_id=device, device_id_type=MESH
        )

    def fetch(src, dst, i):
        return pltpu.make_async_copy(src, dst, load.at[i])

    barrier = pltpu.get_barrier_semaphore()
    for k in range(1, 16):
        pl.semaphore_signal(barrier, inc=1, device_id=in_plane(k), device_id_type=MESH)
        pl.semaphore_signal(barrier, inc=1, device_id=column(k), device_id_type=MESH)

    fetches = [
        fetch(w_h.at[:, pl.ds(own, half)], w_own, 0),
        fetch(g_h.at[0, :, pl.ds(own, half)], g_own, 1),
        fetch(w_h.at[:, pl.ds(oth, half)], w_oth, 2),
        fetch(g_h.at[0, :, pl.ds(oth, half)], g_oth, 3),
        fetch(f_h.at[:, 0, :], fv, 4),
        fetch(s_h.at[:, 0, :], sv, 5),
    ]
    for f in fetches:
        f.start()


    def rows_of(i):
        return pl.ds(pl.multiple_of(i * ROWS, ROWS), ROWS)

    def bulk1(hop, i):
        at = rows_of(i)
        src = ring1.at[hop - 1, at] if hop else g_h.at[0, at, pl.ds(oth, half)]
        return remote(src, ring1.at[hop, at], b1s.at[hop], b1r.at[hop, i], onward)

    def bulk2(hop, i):
        at = rows_of(i)
        sent = pl.ds(SPARE, half - SPARE)
        src = ring2.at[hop - 1, at, sent] if hop else raw.at[at, sent]
        return remote(src, ring2.at[hop, at, sent], b2s.at[hop], b2r.at[hop, i], onward)

    def forward(bulk, hop, low, high):
        def one(i):
            bulk(hop - 1, i).wait_recv()
            bulk(hop, i).start()

        each(low, high, one)

    fetches[0].wait()
    fetches[1].wait()

    def own_sums(b):
        at = pl.ds(pl.multiple_of(b * BLK, BLK), BLK)
        w = w_own[:, at]
        st[b, dp] = jnp.sum(w * g_own[:, at], axis=0, keepdims=True)
        st[b, 2] = jnp.sum(w * w, axis=0, keepdims=True)

    each(0, blocks, own_sums)
    fetches[2].wait()
    fetches[3].wait()

    def other_sums(b):
        at = pl.ds(pl.multiple_of(b * BLK, BLK), BLK)
        st[b, 1 - dp] = jnp.sum(w_oth[:, at] * g_oth[:, at], axis=0, keepdims=True)

    each(0, blocks, other_sums)
    pl.semaphore_wait(barrier, 30)

    each(0, chunks, lambda i: bulk1(0, i).start())

    def scatter(src, dst, stage):
        def copy(k):
            to = lax.rem(q + k, PLANE)
            return remote(src.at[to], dst.at[q], small_s.at[stage], small_r.at[stage], in_plane(k))

        return copy

    def gather(ref, stage):
        def copy(k):
            return remote(ref.at[q], ref.at[q], small_s.at[stage], small_r.at[stage], in_plane(k))

        return copy

    def messages(ref, count, stage):
        every = ref.at[pl.ds(0, count)]
        return remote(every, every, small_s.at[stage], small_r.at[stage], onward)

    rs[q] = st[q]
    scatter1 = scatter(st, rs, 0)
    each(1, PLANE, lambda k: scatter1(k).start())
    messages(rs, 15, 0).wait_recv()
    col[u, 0:3] = jnp.sum(rs[...], axis=0)
    for hop in range(1, HOPS):
        forward(bulk1, hop, 0, chunks)

    def add_up(i, total):
        bulk1(HOPS - 1, i).wait_recv()
        at = rows_of(i)
        for b in range(blocks):
            cols = pl.ds(b * BLK, BLK)
            p = g_own[at, cols] + ring1[HOPS - 1, at, cols]
            grad[at, cols] = p
            total = total + p * p
        return total

    total = lax.fori_loop(0, chunks, add_up, jnp.zeros((ROWS, BLK), F32))
    col[u, 3] = jnp.sum(total, axis=0, keepdims=True)

    def gather_z(k):
        return remote(col.at[u], col.at[u], small_s.at[1], small_r.at[1], column(k))

    for k in range(1, 16):
        gather_z(k).start()
    fetches[4].wait()
    fetches[5].wait()
    norms[...] = jnp.zeros_like(norms)
    messages(col, 15, 1).wait_recv()
    total = jnp.zeros((1, BLK), F32)
    for core in range(2):
        parts = [jnp.sum(col[pl.ds(core * 8 + h * Z_LO, Z_LO)], axis=0) for h in range(2)]
        for h in range(2):
            inner = parts[0][h] + parts[1][h]
            ratio[core, h] = inner / parts[h][2]
            total += parts[h][3] - inner * ratio[core, h]
    plane[q, 0] = ratio[lat, dp]
    plane[q, 1] = ratio[lat, 1 - dp]
    plane[q, 2] = total
    gather1 = gather(plane, 2)
    for k in range(1, PLANE):
        gather1(k).start()

    def spare_copy(i):
        src = (grad, fv, sv)[i].at[:, pl.ds(0, SPARE)]
        return remote(src, spare.at[i], spare_s, spare_r, partner)

    for i in range(3):
        spare_copy(i).start()
    messages(plane, 15, 2).wait_recv()
    total = jnp.sum(jnp.sum(plane[:, 2], axis=0), axis=1, keepdims=True)
    total = jnp.maximum(total, 0.0)
    clip = jnp.minimum(F32(1.0), 0.5 / jnp.sqrt(total / entries + 1e-06))

    def step_of(g, ratios, w, f, s):
        clipped = clip * (g - ratios * w)
        new_f = 0.9 * f + 0.1 * clipped
        new_s = 0.999 * s + 0.001 * clipped * clipped
        return new_f, new_s, w - 0.2 * new_f / (jnp.sqrt(new_s) + 1e-08)

    def update(i):
        at = rows_of(i)
        for b in range(blocks):
            cols = pl.ds(b * BLK, BLK)
            first, second, r = step_of(
                grad[at, cols], plane[b, 0], w_own[at, cols], fv[at, cols], sv[at, cols]
            )
            nf[at, cols] = first
            ns[at, cols] = second
            raw[at, cols] = r
            norms[:, cols] += r * r
        bulk2(0, i).start()

    each(0, chunks, update)
    for b in range(blocks):
        cst[b] = jnp.sum(norms[:, pl.ds(b * BLK, BLK)], axis=0, keepdims=True)

    pn[q] = cst[q]
    scatter2 = scatter(cst, pn, 3)
    each(1, PLANE, lambda k: scatter2(k).start())
    messages(pn, 15, 3).wait_recv()
    zn[z8] = jnp.sum(pn[...], axis=0)

    def gather_n(k):
        return remote(zn.at[z8], zn.at[z8], small_s.at[4], small_r.at[4], along_z(k))

    each(1, 8, lambda k: gather_n(k).start())
    forward(bulk2, 1, 0, chunks)
    forward(bulk2, 2, 0, chunks // 2)
    messages(zn, 7, 4).wait_recv()
    for h in range(2):
        scale[q, h] = lax.rsqrt(jnp.sum(zn[h * Z_LO : (h + 1) * Z_LO], axis=0) / depth + 1e-06)
    gather2 = gather(scale, 5)
    each(1, PLANE, lambda k: gather2(k).start())
    forward(bulk2, 2, chunks // 2, chunks)
    messages(scale, 15, 5).wait_recv()

    def finish(src, part, base):
        def step(i):
            at = rows_of(i)
            for b in range(blocks):
                cols = pl.ds(pl.multiple_of(base + b * BLK, BLK), BLK)
                nw[at, cols] = src[at, pl.ds(b * BLK, BLK)] * scale[b, part]

        return step

    remote(spare, spare, spare_s, spare_r, partner).wait_recv()

    def update_spare(i):
        at = rows_of(i)
        cols = pl.ds(0, SPARE)
        ring2[HOPS - 1, at, cols] = step_of(
            spare[0, at], plane[0, 1][:, :SPARE], w_oth[at, cols], spare[1, at], spare[2, at]
        )[2]

    each(0, chunks, update_spare)
    each(0, chunks, finish(raw, dp, own))
    forward(bulk2, 3, 0, chunks)
    last = finish(ring2.at[HOPS - 1], 1 - dp, oth)

    def receive(i):
        bulk2(HOPS - 1, i).wait_recv()
        last(i)

    def sent(ref, sems, hop):
        return remote(ref, ref, sems.at[hop], b1r.at[hop, 0], onward)

    for hop in range(HOPS):
        sent(ring1.at[hop], b1s, hop).wait_send()
    for hop in range(HOPS - 1):
        sent(ring2.at[hop, :, pl.ds(SPARE, half - SPARE)], b2s, hop).wait_send()
    for stage, (ref, count) in enumerate(((rs, 15), (col, 15), (plane, 15), (pn, 15), (zn, 7), (scale, 15))):
        messages(ref, count, stage).wait_send()
    remote(spare, spare, spare_s, spare_r, partner).wait_send()
    each(0, chunks, receive)
    sent(ring2.at[HOPS - 1, :, pl.ds(SPARE, half - SPARE)], b2s, HOPS - 1).wait_send()


def store(nw, nf, ns, nw_h, nf_h, ns_h, sem):
    copies = [
        pltpu.make_async_copy(nw, nw_h, sem.at[0]),
        pltpu.make_async_copy(nf, nf_h.at[:, 0, :], sem.at[1]),
        pltpu.make_async_copy(ns, ns_h.at[:, 0, :], sem.at[2]),
    ]
    for c in copies:
        c.start()
    for c in copies:
        c.wait()


def solution(mesh):
    def step(weight, grads, first, second):
        rows, width = weight.shape
        half = width // mesh.shape["dp"]
        depth = rows * mesh.shape["row"]
        entries = depth * width * mesh.shape["lat"]
        vmem = pl.BlockSpec(memory_space=pltpu.VMEM)
        hbm = pl.BlockSpec(memory_space=pltpu.HBM)
        tile = pltpu.VMEM((rows, half), F32)
        chunks = rows // ROWS
        dma = pltpu.SemaphoreType.DMA
        new_weight, new_first, new_second = pl.pallas_call(
            functools.partial(comm, depth, entries),
            out_shape=(
                jax.ShapeDtypeStruct((rows, width), F32),
                jax.ShapeDtypeStruct((rows, half), F32),
                jax.ShapeDtypeStruct((rows, half), F32),
            ),
            in_specs=[hbm] * 4,
            out_specs=[vmem] * 3,
            scratch_shapes=[
                *[tile] * 8,
                pltpu.VMEM((ROWS, half), F32),
                pltpu.VMEM((HOPS, rows, half), F32),
                pltpu.VMEM((HOPS, rows, half), F32),
                pltpu.VMEM((PLANE, 3, 1, BLK), F32),
                pltpu.VMEM((PLANE, 3, 1, BLK), F32),
                pltpu.VMEM((16, 4, 1, BLK), F32),
                pltpu.VMEM((2, 2, 1, BLK), F32),
                pltpu.VMEM((PLANE, 3, 1, BLK), F32),
                pltpu.VMEM((PLANE, 1, BLK), F32),
                pltpu.VMEM((PLANE, 1, BLK), F32),
                pltpu.VMEM((8, 1, BLK), F32),
                pltpu.VMEM((PLANE, 2, 1, BLK), F32),
                pltpu.VMEM((3, rows, SPARE), F32),
                dma((6,)),
                dma((HOPS,)),
                dma((HOPS, chunks)),
                dma((HOPS,)),
                dma((HOPS, chunks)),
                dma((6,)),
                dma((6,)),
                dma,
                dma,
            ],
            compiler_params=pltpu.CompilerParams(
                collective_id=0, has_side_effects=True, vmem_limit_bytes=32 << 20
            ),
        )(*[pltpu.with_memory_space_constraint(a, pltpu.HBM) for a in (weight, grads, first, second)])
        return pl.pallas_call(
            store,
            out_shape=(
                jax.ShapeDtypeStruct(weight.shape, F32),
                jax.ShapeDtypeStruct(first.shape, F32),
                jax.ShapeDtypeStruct(second.shape, F32),
            ),
            in_specs=[vmem] * 3,
            out_specs=[hbm] * 3,
            scratch_shapes=[dma((3,))],
            compiler_params=pltpu.CompilerParams(vmem_limit_bytes=16 << 20),
        )(new_weight, new_first, new_second)

    return jax.shard_map(
        step,
        mesh=mesh,
        in_specs=(P("row", "lat"), P("dp", "row", "lat"), P("row", "dp", "lat"), P("row", "dp", "lat")),
        out_specs=(P("row", "lat"), P("row", "dp", "lat"), P("row", "dp", "lat")),
        check_vma=False,
    )
```

```python
import functools

import jax
import jax.numpy as jnp
from jax import lax
from jax.experimental import pallas as pl
from jax.experimental.pallas import tpu as pltpu
from jax.sharding import PartitionSpec as P

MESH = pl.DeviceIdType.MESH
F32 = jnp.float32
PLANE = 16
Z_LO = 4
BLK = 256
ROWS = 16
HOPS = 4
PLANE_ORDER = (10, 6, 14, 9, 11, 2, 8, 5, 7, 13, 15, 1, 3, 4, 12)
COLUMN_ORDER = (4, 12, 3, 5, 11, 13, 2, 6, 10, 14, 1, 7, 9, 15, 8)
SPARE = 128

def each(low, high, body):
    def step(k, carry):
        body(k)
        return carry

    lax.fori_loop(low, high, step, 0)


def comm(
    depth, entries, w_h, g_h, f_h, s_h, nw, nf, ns,
    w_own, w_oth, g_own, g_oth, fv, sv, grad, raw, norms, ring1, ring2,
    st, rs, col, ratio, plane, cst, pn, zn, scale, spare,
    load, b1s, b1r, b2s, b2r, small_s, small_r, spare_s, spare_r,
):
    rows, half = w_own.shape
    chunks, blocks = rows // ROWS, half // BLK
    dp, lat, row = lax.axis_index("dp"), lax.axis_index("lat"), lax.axis_index("row")
    zlo, q = row // PLANE, lax.rem(row, PLANE)
    z8 = dp * Z_LO + zlo
    u = lat * 8 + z8
    own = pl.multiple_of(dp * half, half)
    oth = pl.multiple_of((1 - dp) * half, half)

    def in_plane(k):
        return (dp, lat, zlo * PLANE + lax.rem(q + k, PLANE))

    def column(k):
        v = lax.rem(u + k, 16)
        z = lax.rem(v, 8)
        return (z // Z_LO, v // 8, lax.rem(z, Z_LO) * PLANE + q)

    def along_z(k):
        z = lax.rem(z8 + k, 8)
        return (z // Z_LO, lat, lax.rem(z, Z_LO) * PLANE + q)

    onward = along_z(1 + 6 * lat)
    partner = along_z(HOPS)

    def remote(src, dst, s, r, device):
        return pltpu.make_async_remote_copy(
            src_ref=src, dst_ref=dst, send_sem=s, recv_sem=r, device_id=device, device_id_type=MESH
        )

    def fetch(src, dst, i):
        return pltpu.make_async_copy(src, dst, load.at[i])

    barrier = pltpu.get_barrier_semaphore()
    for k, j in zip(PLANE_ORDER, COLUMN_ORDER):
        pl.semaphore_signal(barrier, inc=1, device_id=in_plane(k), device_id_type=MESH)
        pl.semaphore_signal(barrier, inc=1, device_id=column(j), device_id_type=MESH)

    fetches = [
        fetch(w_h.at[:, pl.ds(own, half)], w_own, 0),
        fetch(g_h.at[0, :, pl.ds(own, half)], g_own, 1),
        fetch(w_h.at[:, pl.ds(oth, half)], w_oth, 2),
        fetch(g_h.at[0, :, pl.ds(oth, half)], g_oth, 3),
        fetch(f_h.at[:, 0, :], fv, 4),
        fetch(s_h.at[:, 0, :], sv, 5),
    ]
    for f in fetches:
        f.start()


    def rows_of(i):
        return pl.ds(pl.multiple_of(i * ROWS, ROWS), ROWS)

    def bulk1(hop, i):
        at = rows_of(i)
        src = ring1.at[hop - 1, at] if hop else g_h.at[0, at, pl.ds(oth, half)]
        return remote(src, ring1.at[hop, at], b1s.at[hop], b1r.at[hop, i], onward)

    def bulk2(hop, i):
        at = rows_of(i)
        sent = pl.ds(SPARE, half - SPARE)
        src = ring2.at[hop - 1, at, sent] if hop else raw.at[at, sent]
        return remote(src, ring2.at[hop, at, sent], b2s.at[hop], b2r.at[hop, i], onward)

    def forward(bulk, hop, low, high):
        def one(i):
            bulk(hop - 1, i).wait_recv()
            bulk(hop, i).start()

        each(low, high, one)

    fetches[0].wait()
    fetches[1].wait()

    def own_sums(b):
        at = pl.ds(pl.multiple_of(b * BLK, BLK), BLK)
        w = w_own[:, at]
        st[b, dp] = jnp.sum(w * g_own[:, at], axis=0, keepdims=True)
        st[b, 2] = jnp.sum(w * w, axis=0, keepdims=True)

    each(0, blocks, own_sums)
    fetches[2].wait()
    fetches[3].wait()

    def other_sums(b):
        at = pl.ds(pl.multiple_of(b * BLK, BLK), BLK)
        st[b, 1 - dp] = jnp.sum(w_oth[:, at] * g_oth[:, at], axis=0, keepdims=True)

    each(0, blocks, other_sums)
    pl.semaphore_wait(barrier, 30)

    each(0, chunks, lambda i: bulk1(0, i).start())

    def scatter(src, dst, stage):
        def copy(k):
            to = lax.rem(q + k, PLANE)
            return remote(src.at[to], dst.at[q], small_s.at[stage], small_r.at[stage], in_plane(k))

        return copy

    def gather(ref, stage):
        def copy(k):
            return remote(ref.at[q], ref.at[q], small_s.at[stage], small_r.at[stage], in_plane(k))

        return copy

    def messages(ref, count, stage):
        every = ref.at[pl.ds(0, count)]
        return remote(every, every, small_s.at[stage], small_r.at[stage], onward)

    rs[q] = st[q]
    scatter1 = scatter(st, rs, 0)
    each(1, PLANE, lambda k: scatter1(k).start())
    messages(rs, 15, 0).wait_recv()
    col[u, 0:3] = jnp.sum(rs[...], axis=0)
    for hop in range(1, HOPS):
        forward(bulk1, hop, 0, chunks)

    def add_up(i, total):
        bulk1(HOPS - 1, i).wait_recv()
        at = rows_of(i)
        for b in range(blocks):
            cols = pl.ds(b * BLK, BLK)
            p = g_own[at, cols] + ring1[HOPS - 1, at, cols]
            grad[at, cols] = p
            total = total + p * p
        return total

    total = lax.fori_loop(0, chunks, add_up, jnp.zeros((ROWS, BLK), F32))
    col[u, 3] = jnp.sum(total, axis=0, keepdims=True)

    def gather_z(k):
        return remote(col.at[u], col.at[u], small_s.at[1], small_r.at[1], column(k))

    for k in COLUMN_ORDER:
        gather_z(k).start()
    fetches[4].wait()
    fetches[5].wait()
    norms[...] = jnp.zeros_like(norms)
    messages(col, 15, 1).wait_recv()
    total = jnp.zeros((1, BLK), F32)
    for core in range(2):
        parts = [jnp.sum(col[pl.ds(core * 8 + h * Z_LO, Z_LO)], axis=0) for h in range(2)]
        for h in range(2):
            inner = parts[0][h] + parts[1][h]
            ratio[core, h] = inner / parts[h][2]
            total += parts[h][3] - inner * ratio[core, h]
    plane[q, 0] = ratio[lat, dp]
    plane[q, 1] = ratio[lat, 1 - dp]
    plane[q, 2] = total
    gather1 = gather(plane, 2)
    for k in PLANE_ORDER:
        gather1(k).start()

    def spare_copy(i):
        src = (grad, fv, sv)[i].at[:, pl.ds(0, SPARE)]
        return remote(src, spare.at[i], spare_s, spare_r, partner)

    for i in range(3):
        spare_copy(i).start()
    messages(plane, 15, 2).wait_recv()
    total = jnp.sum(jnp.sum(plane[:, 2], axis=0), axis=1, keepdims=True)
    total = jnp.maximum(total, 0.0)
    clip = jnp.minimum(F32(1.0), 0.5 / jnp.sqrt(total / entries + 1e-06))

    def step_of(g, ratios, w, f, s):
        clipped = clip * (g - ratios * w)
        new_f = 0.9 * f + 0.1 * clipped
        new_s = 0.999 * s + 0.001 * clipped * clipped
        return new_f, new_s, w - 0.2 * new_f / (jnp.sqrt(new_s) + 1e-08)

    def update(i):
        at = rows_of(i)
        for b in range(blocks):
            cols = pl.ds(b * BLK, BLK)
            first, second, r = step_of(
                grad[at, cols], plane[b, 0], w_own[at, cols], fv[at, cols], sv[at, cols]
            )
            nf[at, cols] = first
            ns[at, cols] = second
            raw[at, cols] = r
            norms[:, cols] += r * r
        bulk2(0, i).start()

    each(0, chunks, update)
    for b in range(blocks):
        cst[b] = jnp.sum(norms[:, pl.ds(b * BLK, BLK)], axis=0, keepdims=True)

    pn[q] = cst[q]
    scatter2 = scatter(cst, pn, 3)
    each(1, PLANE, lambda k: scatter2(k).start())
    messages(pn, 15, 3).wait_recv()
    zn[z8] = jnp.sum(pn[...], axis=0)

    def gather_n(k):
        return remote(zn.at[z8], zn.at[z8], small_s.at[4], small_r.at[4], along_z(k))

    each(1, 8, lambda k: gather_n(k).start())
    forward(bulk2, 1, 0, chunks)
    forward(bulk2, 2, 0, chunks // 2)
    messages(zn, 7, 4).wait_recv()
    for h in range(2):
        scale[q, h] = lax.rsqrt(jnp.sum(zn[h * Z_LO : (h + 1) * Z_LO], axis=0) / depth + 1e-06)
    gather2 = gather(scale, 5)
    each(1, PLANE, lambda k: gather2(k).start())
    forward(bulk2, 2, chunks // 2, chunks)
    messages(scale, 15, 5).wait_recv()

    def finish(src, part, base):
        def step(i):
            at = rows_of(i)
            for b in range(blocks):
                cols = pl.ds(pl.multiple_of(base + b * BLK, BLK), BLK)
                nw[at, cols] = src[at, pl.ds(b * BLK, BLK)] * scale[b, part]

        return step

    remote(spare, spare, spare_s, spare_r, partner).wait_recv()

    def update_spare(i):
        at = rows_of(i)
        cols = pl.ds(0, SPARE)
        ring2[HOPS - 1, at, cols] = step_of(
            spare[0, at], plane[0, 1][:, :SPARE], w_oth[at, cols], spare[1, at], spare[2, at]
        )[2]

    each(0, chunks, update_spare)
    each(0, chunks, finish(raw, dp, own))
    forward(bulk2, 3, 0, chunks)
    last = finish(ring2.at[HOPS - 1], 1 - dp, oth)

    def receive(i):
        bulk2(HOPS - 1, i).wait_recv()
        last(i)

    def sent(ref, sems, hop):
        return remote(ref, ref, sems.at[hop], b1r.at[hop, 0], onward)

    for hop in range(HOPS):
        sent(ring1.at[hop], b1s, hop).wait_send()
    for hop in range(HOPS - 1):
        sent(ring2.at[hop, :, pl.ds(SPARE, half - SPARE)], b2s, hop).wait_send()
    for stage, (ref, count) in enumerate(((rs, 15), (col, 15), (plane, 15), (pn, 15), (zn, 7), (scale, 15))):
        messages(ref, count, stage).wait_send()
    remote(spare, spare, spare_s, spare_r, partner).wait_send()
    each(0, chunks, receive)
    sent(ring2.at[HOPS - 1, :, pl.ds(SPARE, half - SPARE)], b2s, HOPS - 1).wait_send()


def store(nw, nf, ns, nw_h, nf_h, ns_h, sem):
    copies = [
        pltpu.make_async_copy(nw, nw_h, sem.at[0]),
        pltpu.make_async_copy(nf, nf_h.at[:, 0, :], sem.at[1]),
        pltpu.make_async_copy(ns, ns_h.at[:, 0, :], sem.at[2]),
    ]
    for c in copies:
        c.start()
    for c in copies:
        c.wait()


def solution(mesh):
    def step(weight, grads, first, second):
        rows, width = weight.shape
        half = width // mesh.shape["dp"]
        depth = rows * mesh.shape["row"]
        entries = depth * width * mesh.shape["lat"]
        vmem = pl.BlockSpec(memory_space=pltpu.VMEM)
        hbm = pl.BlockSpec(memory_space=pltpu.HBM)
        tile = pltpu.VMEM((rows, half), F32)
        chunks = rows // ROWS
        dma = pltpu.SemaphoreType.DMA
        new_weight, new_first, new_second = pl.pallas_call(
            functools.partial(comm, depth, entries),
            out_shape=(
                jax.ShapeDtypeStruct((rows, width), F32),
                jax.ShapeDtypeStruct((rows, half), F32),
                jax.ShapeDtypeStruct((rows, half), F32),
            ),
            in_specs=[hbm] * 4,
            out_specs=[vmem] * 3,
            scratch_shapes=[
                *[tile] * 8,
                pltpu.VMEM((ROWS, half), F32),
                pltpu.VMEM((HOPS, rows, half), F32),
                pltpu.VMEM((HOPS, rows, half), F32),
                pltpu.VMEM((PLANE, 3, 1, BLK), F32),
                pltpu.VMEM((PLANE, 3, 1, BLK), F32),
                pltpu.VMEM((16, 4, 1, BLK), F32),
                pltpu.VMEM((2, 2, 1, BLK), F32),
                pltpu.VMEM((PLANE, 3, 1, BLK), F32),
                pltpu.VMEM((PLANE, 1, BLK), F32),
                pltpu.VMEM((PLANE, 1, BLK), F32),
                pltpu.VMEM((8, 1, BLK), F32),
                pltpu.VMEM((PLANE, 2, 1, BLK), F32),
                pltpu.VMEM((3, rows, SPARE), F32),
                dma((6,)),
                dma((HOPS,)),
                dma((HOPS, chunks)),
                dma((HOPS,)),
                dma((HOPS, chunks)),
                dma((6,)),
                dma((6,)),
                dma,
                dma,
            ],
            compiler_params=pltpu.CompilerParams(
                collective_id=0, has_side_effects=True, vmem_limit_bytes=32 << 20
            ),
        )(*[pltpu.with_memory_space_constraint(a, pltpu.HBM) for a in (weight, grads, first, second)])
        return pl.pallas_call(
            store,
            out_shape=(
                jax.ShapeDtypeStruct(weight.shape, F32),
                jax.ShapeDtypeStruct(first.shape, F32),
                jax.ShapeDtypeStruct(second.shape, F32),
            ),
            in_specs=[vmem] * 3,
            out_specs=[hbm] * 3,
            scratch_shapes=[dma((3,))],
            compiler_params=pltpu.CompilerParams(vmem_limit_bytes=16 << 20),
        )(new_weight, new_first, new_second)

    return jax.shard_map(
        step,
        mesh=mesh,
        in_specs=(P("row", "lat"), P("dp", "row", "lat"), P("row", "dp", "lat"), P("row", "dp", "lat")),
        out_specs=(P("row", "lat"), P("row", "dp", "lat"), P("row", "dp", "lat")),
        check_vma=False,
    )
```
